128 devices in a mesh: face: 4 (over y), inface: 32 (over x, z, core).
Axes of the slice: x: 4, y: 4, z: 4, core: 2. Of those that a mesh axis runs over, the one named last changes fastest.
Arguments:
- model_state: float32 [4, 58, 524288], P(None, None, ('face', 'inface')), may hold values from -6 to 6
- coupling: float32 [58, 524288], P(None, ('face', 'inface')), may hold values from 0.05 to 20
- cosine: float32 [524288], P(('face', 'inface')), may hold values from 0.15 to 1
- albedo: float32 [524288], P(('face', 'inface')), may hold values from 0.05 to 0.8
- absorb: float32 [14], replicated, may hold values from 0.005 to 0.5
- weights: float32 [14], replicated, may hold values from 0.2 to 1.5
- span_map: int32 [4, 1024], P('face', 'inface'), may hold values from 0 to 1023, as said below
- sunlit: int32 [4, 1024], P('face', 'inface'), may hold values from 0 to 1, as said below
Outputs:
- new_state: float32 [4, 58, 524288], P(None, None, ('face', 'inface'))
- surface_flux: float32 [524288], P(('face', 'inface'))
The draws below stay inside these ranges and needn't reach their ends.
Inputs may be any that keep to these rules, and one draw needn't show every extreme that they name: `span_map`: in each face block the entries are a permutation of the spans; the blocks of one device go to each device of its face block exactly 1 at a time. The sunlit spans of a device and those of the device whose face index differs in bit 1 (same inface index) number 32 together; a device holds at most 28 sunlit spans, and some device exactly 28.
All inputs are finite; a program needn't handle non-finite values.
Results may differ from the reference program's by a relative error of at most 0.000023.
Values sent between devices are 32-bit elements; how exact they have to be, the bound alone decides.
No kernel may reach another device: no remote copies, remote signals or barrier semaphores. Data moves between devices by JAX's collectives and lax.ppermute only.
A program may use at most 64 MiB of HBM per device.

```python
import math
import jax
import jax.numpy as jnp
from jax import lax

LEV = 58
NB = 14
FIELDS = 4
PCOLS = 128
BLK_DEV = 32
SUN_MAX = 28
BLKS_FACE = 1024
COLS = 524288
N_FACE = 4
N_INFACE = 32


def draw_span_map(key, part):
    inface_count = BLKS_FACE // BLK_DEV
    per_owner = BLK_DEV // inface_count
    source_keys = jax.random.split(jax.random.fold_in(key, 11), N_FACE * inface_count)
    target_keys = jax.random.split(jax.random.fold_in(key, 23), N_FACE * inface_count)
    source_perm = jax.vmap(lambda k: jax.random.permutation(k, BLK_DEV))(source_keys).reshape(N_FACE, inface_count, BLK_DEV)
    target_perm = jax.vmap(lambda k: jax.random.permutation(k, BLK_DEV))(target_keys).reshape(N_FACE, inface_count, BLK_DEV)
    owner = source_perm // per_owner
    within = source_perm % per_owner
    face_index = jnp.arange(N_FACE)[:, None, None]
    source_index = jnp.arange(inface_count)[None, :, None]
    slot = target_perm[face_index, owner, source_index * per_owner + within]
    return (owner * BLK_DEV + slot).reshape(N_FACE, BLKS_FACE).astype(jnp.int32)


def draw_sunlit(key, part):
    inface_count = BLKS_FACE // BLK_DEV
    counts = jax.random.randint(jax.random.fold_in(key, 5), (2, inface_count), BLK_DEV - SUN_MAX, SUN_MAX + 1)
    chosen = jax.random.randint(jax.random.fold_in(key, 7), (), 0, 2 * inface_count)
    flat_counts = counts.reshape(-1)
    flat_counts = jnp.where(jnp.arange(2 * inface_count) == chosen, SUN_MAX, flat_counts)
    counts = flat_counts.reshape(2, inface_count)
    all_counts = jnp.concatenate([counts, BLK_DEV - counts], axis=0)
    perm_keys = jax.random.split(jax.random.fold_in(key, 9), N_FACE * inface_count)
    ranks = jax.vmap(lambda k: jax.random.permutation(k, BLK_DEV))(perm_keys).reshape(N_FACE, inface_count, BLK_DEV)
    flags = (ranks < all_counts[:, :, None]).astype(jnp.int32)
    return flags.reshape(N_FACE, BLKS_FACE)


def level_of(own_key, dims, pieces, low, largest):
    def one(dim, blocks):
        steps = jax.random.uniform(jax.random.fold_in(jax.random.fold_in(own_key, 6), dim), (blocks,), jnp.float32, low / len(pieces), largest / len(pieces))
        return jnp.repeat(jnp.exp(steps), dims[dim] // blocks).reshape((-1,) + (1,) * (len(dims) - dim - 1))

    level = one(*pieces[0])
    for cut in pieces[1:]:
        level = level * one(*cut)
    return level


def scatter_about(stream_key, shape, spread, reach, cuts=(), held_as=jnp.bfloat16):
    level = level_of(stream_key, shape, cuts, -0.22, 0.18) if cuts else 1.0
    array = jax.random.normal(stream_key, shape, jnp.float32) * spread * level
    return jnp.minimum(jnp.maximum(array, -reach), reach).astype(held_as)


def setup_inputs(seed: int = 0) -> dict:
    keys = jax.random.split(jax.random.key(seed), 9)
    model_state = scatter_about(keys[0], (FIELDS, LEV, COLS), 1.0, 6.0, ((2, 128),), jnp.float32)
    coupling = jnp.clip(jnp.exp(math.log(20.0) - 5.9914645 * jax.random.uniform(keys[1], (LEV, COLS), jnp.float32) ** level_of(keys[1], (LEV, COLS), ((1, 128),), -0.2, 0.2)), 0.05, 20.0)
    cosine = jnp.clip(0.15 + 0.85 * jax.random.uniform(keys[2], (COLS,), jnp.float32) ** level_of(keys[2], (COLS,), ((0, 128),), -0.2, 0.2), 0.15, 1.0)
    albedo = jnp.clip(0.05 + 0.75 * jax.random.uniform(keys[3], (COLS,), jnp.float32) ** level_of(keys[3], (COLS,), ((0, 128),), -0.2, 0.2), 0.05, 0.8)
    absorb = jnp.clip(jnp.exp(jax.random.uniform(keys[4], (NB,), jnp.float32, math.log(0.005), math.log(0.5))), 0.005, 0.5)
    weights = jnp.clip(jnp.exp(jax.random.uniform(keys[5], (NB,), jnp.float32, math.log(0.2), math.log(1.5))), 0.2, 1.5)
    span_map = draw_span_map(jax.random.fold_in(keys[8], 71), 0)
    sunlit = draw_sunlit(jax.random.fold_in(keys[8], 71), 0)
    return dict(model_state=model_state, coupling=coupling, cosine=cosine, albedo=albedo, absorb=absorb, weights=weights, span_map=span_map, sunlit=sunlit)


def vertical_solve(source_rows, coupling):
    levels = source_rows.shape[1]
    gains = []
    partial_values = []
    for level_index in range(levels):
        below = coupling[level_index]
        if level_index == 0:
            divisor = 1.0 + below
            current = source_rows[:, 0]
        else:
            above = coupling[level_index - 1]
            divisor = 1.0 + below + above - above * gains[-1]
            current = source_rows[:, level_index] + above * partial_values[-1]
        gains.append(below / divisor)
        partial_values.append(current / divisor)
    solved = [partial_values[-1]]
    for level_index in range(levels - 2, -1, -1):
        solved.append(partial_values[level_index] + gains[level_index] * solved[-1])
    return jnp.stack(solved[::-1], axis=1)


def two_stream(moisture, cosine, albedo, absorb, weights):
    levels = moisture.shape[0]
    down_flux = [weights[:, None] * cosine[None, :]]
    transmit = []
    reflect = []
    for level_index in range(levels):
        optical = absorb[:, None] * (1.2 + jnp.tanh(moisture[level_index]))[None, :]
        passed = jnp.exp(-optical / cosine[None, :])
        transmit.append(passed)
        reflect.append(0.3 * (1.0 - passed))
        down_flux.append(down_flux[-1] * passed)
    up_flux = [None] * (levels + 1)
    up_flux[levels] = albedo[None, :] * down_flux[levels]
    for level_index in range(levels - 1, -1, -1):
        up_flux[level_index] = up_flux[level_index + 1] * transmit[level_index] + reflect[level_index] * down_flux[level_index]
    heating = jnp.stack([5.0 * jnp.sum(down_flux[k] - down_flux[k + 1] + up_flux[k + 1] - up_flux[k], axis=0) for k in range(levels)], axis=0)
    surface = jnp.sum((1.0 - albedo)[None, :] * down_flux[levels], axis=0)
    return heating, surface


def reference(model_state, coupling, cosine, albedo, absorb, weights, span_map, sunlit):
    groups = N_FACE * N_INFACE
    columns = BLK_DEV * PCOLS
    grouped_state = model_state.reshape(FIELDS, LEV, groups, columns).transpose(2, 0, 1, 3)
    grouped_coupling = coupling.reshape(LEV, groups, columns).transpose(1, 0, 2)

    def solve_group(operands):
        return vertical_solve(operands[0], operands[1])

    diffused = lax.map(solve_group, (grouped_state, grouped_coupling))
    diffused = diffused.transpose(1, 2, 0, 3).reshape(FIELDS, LEV, N_FACE, BLKS_FACE, PCOLS)
    face_rows = jnp.arange(N_FACE)[:, None]
    moisture = jnp.zeros((LEV, N_FACE, BLKS_FACE, PCOLS), jnp.float32).at[:, face_rows, span_map].set(diffused[1])
    grouped_moisture = moisture.reshape(LEV, groups, columns).transpose(1, 0, 2)

    def radiate_group(operands):
        return two_stream(operands[0], operands[1], operands[2], absorb, weights)

    heating, surface = lax.map(radiate_group, (grouped_moisture, cosine.reshape(groups, columns), albedo.reshape(groups, columns)))
    flags = jnp.repeat(sunlit.astype(jnp.float32), PCOLS, axis=1).reshape(groups, columns)
    heating = heating * flags[:, None, :]
    surface = surface * flags
    heating = heating.transpose(1, 0, 2).reshape(LEV, N_FACE, BLKS_FACE, PCOLS)
    heating_home = heating[:, face_rows, span_map]
    new_state = diffused.at[0].add(heating_home)
    return new_state.reshape(FIELDS, LEV, COLS), surface.reshape(COLS)
```

```python
import functools

import jax
import jax.numpy as jnp
from jax import lax
from jax.experimental import pallas as pl
from jax.experimental.pallas import tpu as pltpu
from jax.sharding import PartitionSpec as P

LANES = 128
GROUP = 1024
ROWS = 72
LOG2E = 1.4426950408889634
HBM = pl.BlockSpec(memory_space=pl.ANY)
VMEM = pl.BlockSpec(memory_space=pltpu.VMEM)
SMEM = pl.BlockSpec(memory_space=pltpu.SMEM)


def forward_sweep(coupling_ref, field_refs):
    levels, columns = coupling_ref.shape
    zero = jnp.zeros((1, columns), jnp.float32)

    def step(level, carry):
        above, gain, partials = carry
        row = pl.ds(level, 1)
        below = coupling_ref[row, :]
        inverse = 1.0 / (1.0 + below + above - above * gain)
        gain = below * inverse
        partials = tuple(
            (ref[row, :] + above * partial) * inverse for ref, partial in zip(field_refs, partials)
        )
        coupling_ref[row, :] = gain
        for ref, partial in zip(field_refs, partials):
            ref[row, :] = partial
        return below, gain, partials

    lax.fori_loop(0, levels, step, (zero, zero, (zero,) * len(field_refs)), unroll=2)


def first_kernel(
    state_ref, coupling_ref, cosine_ref, albedo_ref, sunlit_ref, map_ref,
    new_ref, optical_ref, send_ref,
    coupling_v, moist_v, total_v, sems,
):
    levels, columns = coupling_ref.shape
    spans = columns // LANES
    peers = send_ref.shape[0]
    loads = [
        pltpu.make_async_copy(coupling_ref, coupling_v, sems.at[0]),
        pltpu.make_async_copy(state_ref.at[1], moist_v, sems.at[1]),
    ]
    for load in loads:
        load.start()
    for span in range(spans):
        lit = sunlit_ref[0, span].astype(jnp.float32)
        send_ref[0, span : span + 1, :] = cosine_ref[span : span + 1, :] * lit
    send_ref[0, spans : 2 * spans, :] = albedo_ref[...]
    for peer in range(1, peers):
        send_ref[peer, : 2 * spans, :] = send_ref[0, : 2 * spans, :]
    for peer in range(peers):
        send_ref[peer, 2 * spans :, :] = jnp.zeros((ROWS - 2 * spans, LANES), jnp.float32)
    for load in loads:
        load.wait()
    forward_sweep(coupling_v, (moist_v,))
    zero = jnp.zeros((1, columns), jnp.float32)

    def back(index, carry):
        value, total = carry
        row = pl.ds(levels - 1 - index, 1)
        value = moist_v[row, :] + coupling_v[row, :] * value
        moist_v[row, :] = value
        optical = 1.2 + jnp.tanh(value)
        optical_ref[levels - 1 - index] = optical
        return value, total + optical

    value, total = lax.fori_loop(0, levels, back, (zero, zero), unroll=2)
    store = pltpu.make_async_copy(moist_v, new_ref.at[1], sems.at[0])
    store.start()
    total_v[...] = total
    for block in range(spans):
        target = map_ref[0, block]
        owner = target // spans
        peer = owner // 2
        core = owner % 2
        slot = (target % spans).astype(jnp.float32)
        send_ref[peer, pl.ds(2 * spans + core, 1), :] = total_v[:, block * LANES : (block + 1) * LANES]
        send_ref[peer, pl.ds(2 * spans + 2 + core, 1), :] = jnp.full((1, LANES), slot, jnp.float32)
    store.wait()


def rest_kernel(state_ref, coupling_ref, _, new_ref, coupling_v, fields_v, sems):
    levels, columns = coupling_ref.shape
    loads = [pltpu.make_async_copy(coupling_ref, coupling_v, sems.at[0])]
    for place, field in enumerate((0, 2, 3)):
        loads.append(pltpu.make_async_copy(state_ref.at[field], fields_v.at[place], sems.at[1 + place]))
    for load in loads:
        load.start()
    for load in loads:
        load.wait()
    forward_sweep(coupling_v, tuple(fields_v.at[place] for place in range(3)))
    zero = jnp.zeros((1, columns), jnp.float32)

    def back(index, values):
        row = pl.ds(levels - 1 - index, 1)
        gain = coupling_v[row, :]
        values = tuple(fields_v[place, row, :] + gain * value for place, value in enumerate(values))
        for place, value in enumerate(values):
            fields_v[place, row, :] = value
        return values

    lax.fori_loop(0, levels, back, (zero,) * 3, unroll=2)
    stores = [
        pltpu.make_async_copy(fields_v.at[place], new_ref.at[field], sems.at[place])
        for place, field in enumerate((0, 2, 3))
    ]
    for store in stores:
        store.start()
    for store in stores:
        store.wait()


def radiate_kernel(
    mine_ref, other_ref, optical_ref, absorb_ref, weights_ref, map_ref, _,
    new_ref, surface_ref,
    table_v, optical_v, first_v, cosine_v, albedo_v, down_v, sums_v, sems,
):
    levels, columns = first_v.shape
    bands = absorb_ref.shape[0]
    spans = columns // LANES
    peers = mine_ref.shape[0]
    groups = columns // GROUP
    me = lax.axis_index("inface")
    core = lax.rem(me, 2)
    loads = [
        pltpu.make_async_copy(mine_ref, table_v.at[core], sems.at[0]),
        pltpu.make_async_copy(other_ref, table_v.at[1 - core], sems.at[1]),
        pltpu.make_async_copy(optical_ref, optical_v, sems.at[2]),
        pltpu.make_async_copy(new_ref.at[0], first_v, sems.at[3]),
    ]
    for load in loads:
        load.start()
    loads[0].wait()
    loads[1].wait()
    for block in range(spans):
        target = map_ref[0, block]
        owner = target // spans
        slot = target % spans
        lanes = slice(block * LANES, (block + 1) * LANES)
        cosine_v[:, lanes] = table_v[owner % 2, owner // 2, pl.ds(slot, 1), :]
        albedo_v[:, lanes] = table_v[owner % 2, owner // 2, pl.ds(spans + slot, 1), :]
    rates = [absorb_ref[band] * (-LOG2E) for band in range(bands)]

    wanted = lax.broadcasted_iota(jnp.int32, (spans, LANES), 0).astype(jnp.float32)
    depth = jnp.zeros((spans, LANES), jnp.float32)
    for half in range(2):
        for peer in range(peers):
            total = table_v[half, peer, pl.ds(2 * spans + core, 1), :]
            slot = table_v[half, peer, pl.ds(2 * spans + 2 + core, 1), :]
            depth = jnp.where(wanted == slot, total, depth)
    own = table_v[core, me // 2, : 2 * spans, :]
    own_cosine = own[:spans]
    lit = own_cosine > 0.0
    depth = jnp.where(lit, depth / jnp.where(lit, own_cosine, 1.0), 0.0)
    flux = jnp.zeros((spans, LANES), jnp.float32)
    for band in range(bands):
        flux = flux + weights_ref[band] * jnp.exp2(rates[band] * depth)
    surface_ref[...] = (1.0 - own[spans:]) * (own_cosine * flux)

    loads[2].wait()
    loads[3].wait()

    def group_step(group, carry):
        lanes = pl.ds(pl.multiple_of(group * GROUP, GROUP), GROUP)
        cosine = cosine_v[:, lanes]
        bright = cosine > 0.0
        inverse = jnp.where(bright, 1.0 / jnp.where(bright, cosine, 1.0), 0.0)
        down = tuple(weights_ref[band] * cosine for band in range(bands))
        top = functools.reduce(jnp.add, down)
        for band in range(bands):
            down_v[0, band] = down[band]

        def descend(level, carry):
            down, above = carry
            optical = optical_v[level, :, lanes] * inverse
            down = tuple(d * jnp.exp2(rate * optical) for d, rate in zip(down, rates))
            for band in range(bands):
                down_v[level + 1, band] = down[band]
            total = functools.reduce(jnp.add, down)
            sums_v[level] = above - total
            return down, total

        down, _ = lax.fori_loop(0, levels, descend, (down, top))
        bounce = albedo_v[:, lanes] * (1.0 / 0.3)
        up = tuple(bounce * d for d in down)

        def ascend(index, carry):
            up, down, below = carry
            level = levels - 1 - index
            optical = optical_v[level, :, lanes] * inverse
            arriving = tuple(down_v[level, band] for band in range(bands))
            up = tuple(
                u * jnp.exp2(rate * optical) + (a - d) for u, rate, a, d in zip(up, rates, arriving, down)
            )
            total = functools.reduce(jnp.add, up)
            row = pl.ds(level, 1)
            first_v[row, lanes] += 5.0 * sums_v[level] + 1.5 * (below - total)
            return up, arriving, total

        lax.fori_loop(0, levels, ascend, (up, down, functools.reduce(jnp.add, up)))
        return carry

    lax.fori_loop(0, groups, group_step, 0)
    store = pltpu.make_async_copy(first_v, new_ref.at[0], sems.at[0])
    store.start()
    store.wait()


def body(model_state, coupling, cosine, albedo, absorb, weights, span_map, sunlit):
    fields, levels, columns = model_state.shape
    spans = columns // LANES
    members = lax.axis_size("inface")
    peers = members // 2
    f32 = jnp.float32
    state_shape = jax.ShapeDtypeStruct(model_state.shape, f32)

    new_state, optical, send = pl.pallas_call(
        first_kernel,
        out_shape=(
            state_shape,
            jax.ShapeDtypeStruct((levels, 1, columns), f32),
            jax.ShapeDtypeStruct((peers, ROWS, LANES), f32),
        ),
        in_specs=[HBM, HBM, VMEM, VMEM, SMEM, SMEM],
        out_specs=(HBM, VMEM, VMEM),
        scratch_shapes=[
            pltpu.VMEM((levels, columns), f32),
            pltpu.VMEM((levels, columns), f32),
            pltpu.VMEM((1, columns), f32),
            pltpu.SemaphoreType.DMA((2,)),
        ],
        name="solve_moisture",
    )(model_state, coupling, cosine.reshape(spans, LANES), albedo.reshape(spans, LANES), sunlit, span_map)

    same_core = [[2 * peer + core for peer in range(peers)] for core in range(2)]
    mine = lax.all_to_all(send, "inface", 0, 0, tiled=True, axis_index_groups=same_core)

    new_state = pl.pallas_call(
        rest_kernel,
        out_shape=state_shape,
        in_specs=[HBM, HBM, HBM],
        out_specs=HBM,
        input_output_aliases={2: 0},
        scratch_shapes=[
            pltpu.VMEM((levels, columns), f32),
            pltpu.VMEM((3, levels, columns), f32),
            pltpu.SemaphoreType.DMA((4,)),
        ],
        name="solve_rest",
        cost_estimate=pl.CostEstimate(flops=20_000_000, bytes_accessed=7_000_000, transcendentals=0),
    )(model_state, coupling, new_state)

    other = lax.ppermute(mine, "inface", [(member, member ^ 1) for member in range(members)])

    new_state, surface = pl.pallas_call(
        radiate_kernel,
        out_shape=(state_shape, jax.ShapeDtypeStruct((spans, LANES), f32)),
        in_specs=[HBM, HBM, HBM, SMEM, SMEM, SMEM, HBM],
        out_specs=(HBM, VMEM),
        input_output_aliases={6: 0},
        scratch_shapes=[
            pltpu.VMEM((2, peers, ROWS, LANES), f32),
            pltpu.VMEM((levels, 1, columns), f32),
            pltpu.VMEM((levels, columns), f32),
            pltpu.VMEM((1, columns), f32),
            pltpu.VMEM((1, columns), f32),
            pltpu.VMEM((levels + 1, absorb.shape[0], 1, GROUP), f32),
            pltpu.VMEM((levels, 1, GROUP), f32),
            pltpu.SemaphoreType.DMA((4,)),
        ],
        name="radiate",
    )(mine, other, optical, absorb, weights, span_map, new_state)
    return new_state, surface.reshape(columns)


def solution(mesh):
    in_specs = (
        P(None, None, ("face", "inface")),
        P(None, ("face", "inface")),
        P(("face", "inface")),
        P(("face", "inface")),
        P(),
        P(),
        P("face", "inface"),
        P("face", "inface"),
    )
    out_specs = (P(None, None, ("face", "inface")), P(("face", "inface")))
    return jax.shard_map(body, mesh=mesh, in_specs=in_specs, out_specs=out_specs, check_vma=False)
```
